32 devices in a mesh: band: 4 (over z), roster: 8 (over y, x, core).
Axes of the slice: x: 2, y: 2, z: 4, core: 2. Of those that a mesh axis runs over, the one named last changes fastest.
Arguments:
- tiles: bfloat16 [4, 8, 6, 256, 256], P('band', 'roster'), as said below
- tile_slots: int32 [4, 8, 6], P('band', 'roster'), may hold values from 0 to 5, each once within a row
- tile_count: int32 [4, 8], P('band', 'roster'), may hold values from 1 to 6, as said below
- costs: float32 [6144, 128], P('roster'), may hold values from 1000 to 10000
- primal_start: float32 [6144, 128], P('roster'), may hold values from 0 to 1
- dual_start: float32 [2048, 128], P('band'), may hold values from 0.5 to 4
Outputs:
- primal: float32 [6144, 128], P('roster')
- dual: float32 [2048, 128], P('band')
The draws below stay inside these ranges and needn't reach their ends.
Inputs may be any that keep to these rules, and one draw needn't show every extreme that they name: `tile_slots`: each device's slots list every tile position once; slot s is in use where s < tile_count. `tile_count`: some device uses all 6 slots. `tiles`: entries are zero or positive.
All inputs are finite; a program needn't handle non-finite values.
Results may differ from the reference program's by a relative error of at most 0.0003.
Values sent between devices are 32-bit elements; how exact they have to be, the bound alone decides.
A program may use at most 64 MiB of HBM per device.

```python
import math
import jax
import jax.numpy as jnp
from jax import lax

TILE = 256
SCEN = 128
ROUNDS = 3
ITERS = 4
TILES_DEV = 6
ROWS_DEV = 512
COLS_DEV = 768
DUTIES = 2048
ROSTERS = 6144
N_BAND = 4
N_ROSTER = 8


def draw_tiles(key, part):
    key_mask, key_value, key_row, key_col = jax.random.split(jax.random.fold_in(key, 11), 4)
    shape = (N_BAND, N_ROSTER, TILES_DEV, TILE, TILE)
    present = jax.random.bernoulli(key_mask, 0.35, shape).astype(jnp.float32)
    value = jnp.exp(jax.random.uniform(key_value, shape, jnp.float32, -0.7, 0.7))
    row_fac = jnp.exp(jax.random.uniform(key_row, (N_BAND, N_ROSTER, TILES_DEV, TILE, 1), jnp.float32, 0.0, math.log(10.0)))
    col_fac = jnp.exp(jax.random.uniform(key_col, (N_BAND, N_ROSTER, TILES_DEV, 1, TILE), jnp.float32, 0.0, math.log(10.0)))
    return (present * value * row_fac * col_fac).astype(jnp.bfloat16)


def draw_tile_count(key, part):
    key_count, key_full, key_other = jax.random.split(jax.random.fold_in(key, 23), 3)
    lowest = max(1, TILES_DEV // 4)
    total = N_BAND * N_ROSTER
    counts = jax.random.randint(key_count, (total,), lowest, TILES_DEV + 1, jnp.int32)
    full_at = jax.random.randint(key_full, (), 0, total, jnp.int32)
    low_at = (full_at + 1 + jax.random.randint(key_other, (), 0, total - 1, jnp.int32)) % total
    counts = counts.at[full_at].set(TILES_DEV).at[low_at].set(lowest)
    return counts.reshape(N_BAND, N_ROSTER)


def levels(stream_key, shape, cuts, least, high):
    level = 1.0
    for axis_at, blocks in cuts:
        steps = jax.random.uniform(jax.random.fold_in(jax.random.fold_in(stream_key, 6), axis_at), (blocks,), jnp.float32, least / len(cuts), high / len(cuts))
        level = level * jnp.repeat(jnp.exp(steps), shape[axis_at] // blocks).reshape((-1,) + (1,) * (len(shape) - 1 - axis_at))
    return level


def setup_inputs(seed: int = 0) -> dict:
    splits = jax.random.split(jax.random.key(seed), 7)
    tiles = draw_tiles(jax.random.fold_in(splits[6], 71), 0)
    tile_slots = jax.vmap(lambda own: jax.random.permutation(own, TILES_DEV))(jax.random.split(splits[1], N_BAND * N_ROSTER)).reshape((N_BAND, N_ROSTER, TILES_DEV)).astype(jnp.int32)
    tile_count = draw_tile_count(jax.random.fold_in(splits[6], 71), 0)
    costs = jnp.clip(jnp.exp(math.log(10000.0) - 2.3025851 * jax.random.uniform(splits[3], (ROSTERS, SCEN), jnp.float32) ** levels(splits[3], (ROSTERS, SCEN), ((0, 8),), -0.2, 0.2)), 1000.0, 10000.0)
    primal_start = jnp.clip(1.0 * jax.random.uniform(splits[4], (ROSTERS, SCEN), jnp.float32) ** levels(splits[4], (ROSTERS, SCEN), ((0, 8),), -0.2, 0.2), 0.0, 1.0)
    dual_start = jnp.clip(0.5 + 3.5 * jax.random.uniform(splits[5], (DUTIES, SCEN), jnp.float32) ** levels(splits[5], (DUTIES, SCEN), ((0, 4),), -0.2, 0.2), 0.5, 4.0)
    return dict(tiles=tiles, tile_slots=tile_slots, tile_count=tile_count, costs=costs, primal_start=primal_start, dual_start=dual_start)


HIGH = lax.Precision.HIGHEST
eps = 1e-06

def block_parts(tile_block, slot_list, count, row_scale, col_scale):
    tile = tile_block.shape[1]
    row_tiles = row_scale.shape[0] // tile
    col_tiles = col_scale.shape[0] // tile
    slots = slot_list.astype(jnp.int32)
    row_index = slots // col_tiles
    col_index = slots % col_tiles
    active = (jnp.arange(slots.shape[0], dtype=jnp.int32) < count).astype(jnp.float32)
    row_part = row_scale.reshape(row_tiles, tile)[row_index]
    col_part = col_scale.reshape(col_tiles, tile)[col_index]
    scaled = tile_block.astype(jnp.float32) * row_part[:, :, None] * col_part[:, None, :] * active[:, None, None]
    row_hot = (row_index[None, :] == jnp.arange(row_tiles, dtype=jnp.int32)[:, None]).astype(jnp.float32)
    col_hot = (col_index[None, :] == jnp.arange(col_tiles, dtype=jnp.int32)[:, None]).astype(jnp.float32)
    return (scaled, row_index, col_index, row_hot, col_hot)

def block_peaks(tile_block, slot_list, count, row_scale, col_scale):
    scaled, row_index, col_index, row_hot, col_hot = block_parts(tile_block, slot_list, count, row_scale, col_scale)
    magnitude = jnp.abs(scaled)
    slot_rows = lax.optimization_barrier(jnp.max(magnitude, axis=2))
    slot_cols = lax.optimization_barrier(jnp.max(magnitude, axis=1))
    row_peak = lax.optimization_barrier(jnp.max(row_hot[:, :, None] * slot_rows[None], axis=1)).reshape(-1)
    col_peak = lax.optimization_barrier(jnp.max(col_hot[:, :, None] * slot_cols[None], axis=1)).reshape(-1)
    return (row_peak, col_peak, jnp.sum(scaled * scaled))

def block_forward(tile_block, slot_list, count, row_scale, col_scale, extrapolated):
    scaled, row_index, col_index, row_hot, col_hot = block_parts(tile_block, slot_list, count, row_scale, col_scale)
    tile = scaled.shape[1]
    gathered = extrapolated.reshape(col_hot.shape[0], tile, -1)[col_index]
    product = jnp.einsum('sij,sjk->sik', scaled, gathered, precision=HIGH)
    return jnp.einsum('rs,sik->rik', row_hot, product, precision=HIGH).reshape(row_scale.shape[0], -1)

def block_backward(tile_block, slot_list, count, row_scale, col_scale, dual_rows):
    scaled, row_index, col_index, row_hot, col_hot = block_parts(tile_block, slot_list, count, row_scale, col_scale)
    tile = scaled.shape[1]
    gathered = dual_rows.reshape(row_hot.shape[0], tile, -1)[row_index]
    product = jnp.einsum('sij,sik->sjk', scaled, gathered, precision=HIGH)
    return jnp.einsum('cs,sjk->cjk', col_hot, product, precision=HIGH).reshape(col_scale.shape[0], -1)

def reference(tiles, tile_slots, tile_count, costs, primal_start, dual_start):
    row_scale = jnp.ones((N_BAND, ROWS_DEV), jnp.float32)
    col_scale = jnp.ones((N_ROSTER, COLS_DEV), jnp.float32)

    def all_peaks(row_scale, col_scale):

        def per_band(items):
            tile_b, slot_b, count_b, rscale_b = items
            return jax.vmap(lambda tb, sl, ct, cs: block_peaks(tb, sl, ct, rscale_b, cs))(tile_b, slot_b, count_b, col_scale)
        return lax.map(per_band, (tiles, tile_slots, tile_count, row_scale))
    for turn in range(ROUNDS):
        row_part, col_part, squares = all_peaks(row_scale, col_scale)
        row_peak = lax.optimization_barrier(jnp.max(row_part, axis=1))
        col_peak = lax.optimization_barrier(jnp.max(col_part, axis=0))
        row_scale = row_scale / jnp.sqrt(row_peak + eps)
        col_scale = col_scale / jnp.sqrt(col_peak + eps)
    row_part, col_part, squares = all_peaks(row_scale, col_scale)
    eta = 0.9 / jnp.sqrt(jnp.sum(squares) + eps)
    col_full = col_scale.reshape(-1)[:, None]
    row_full = row_scale.reshape(-1)[:, None]
    cost_t = costs * col_full
    upper = 1.0 / col_full
    primal = primal_start / col_full
    dual = dual_start / row_full
    for step in range(ITERS):
        dual_bands = dual.reshape(N_BAND, ROWS_DEV, -1)

        def back_step(total, items):
            tile_b, slot_b, count_b, rscale_b, dual_b = items
            terms = jax.vmap(lambda tb, sl, ct, cs: block_backward(tb, sl, ct, rscale_b, cs, dual_b))(tile_b, slot_b, count_b, col_scale)
            return (total + terms, None)
        init = jnp.zeros((N_ROSTER, COLS_DEV, dual.shape[1]), jnp.float32)
        g_whole, unused = lax.scan(back_step, init, (tiles, tile_slots, tile_count, row_scale, dual_bands))
        g_whole = g_whole.reshape(-1, dual.shape[1])
        primal_next = jnp.clip(primal - eta * (cost_t - g_whole), 0.0, upper)
        extrapolated = (2.0 * primal_next - primal).reshape(N_ROSTER, COLS_DEV, -1)

        def per_band(items):
            tile_b, slot_b, count_b, rscale_b = items
            terms = jax.vmap(lambda tb, sl, ct, cs, xb: block_forward(tb, sl, ct, rscale_b, cs, xb))(tile_b, slot_b, count_b, col_scale, extrapolated)
            return lax.optimization_barrier(jnp.sum(terms, axis=0))
        h_whole = lax.map(per_band, (tiles, tile_slots, tile_count, row_scale)).reshape(-1, dual.shape[1])
        dual = dual + eta * (row_full - h_whole)
        primal = primal_next
    return (primal, dual)
```

```python
import functools

import jax
import jax.numpy as jnp
from jax import lax
from jax.experimental import pallas as pl
from jax.experimental.pallas import tpu as pltpu
from jax.sharding import PartitionSpec as P

ROUNDS = 3
ITERS = 4
eps = 1e-06
GROUPS = 1
CHUNK = 16
SKEW = 2
DOWN = 2.0**-24
UP = 2.0**24
MESH = pl.DeviceIdType.MESH
f32 = jnp.float32
bf16 = jnp.bfloat16


def kernel(
    cfg, slots_ref, count_ref, tiles_ref, cost_ref, x0_ref, y0_ref, primal_ref, dual_ref,
    a_ref, at_ref, cost_t, x_t, u_t, y_t, own, snd, rec, hown, hrec,
    rpeak_s, rpeak_r, cpeak_s, cpeak_r, fr_s, fr_r, fb_s, fb_r,
    rp_ss, rp_rs, cp_ss, cp_rs, fr_ss, fr_rs, fb_ss, fb_rs,
    g_ss, g_rs, rs_ss, rs_rs, ag_ss, ag_rs,
):
    nb, nr, groups, cs, skew = cfg
    z = lax.axis_index("band")
    r = lax.axis_index("roster")
    slots = tiles_ref.shape[2]
    tile = tiles_ref.shape[3]
    rows, scen = y0_ref.shape
    cols = cost_ref.shape[0]
    col_tiles = cols // tile
    per = scen // groups
    kper = per // cs
    bs = max(8, per // nr)
    width = per * rows // (nr * bs)
    parts = rows // width

    def roster_peer(d):
        return (z, (r + d) % nr)

    def band_peer(d):
        return ((z + d) % nb, r)

    barrier = pltpu.get_barrier_semaphore()
    for d in range(1, nr):
        pl.semaphore_signal(barrier, inc=1, device_id=roster_peer(d), device_id_type=MESH)
    for d in range(1, nb):
        pl.semaphore_signal(barrier, inc=1, device_id=band_peer(d), device_id_type=MESH)

    for p in range(slots):
        at = jnp.int32(0)
        for s in range(slots):
            at = jnp.where(slots_ref[0, 0, s] == p, jnp.int32(s), at)
        factor = jnp.where(at < count_ref[0, 0], jnp.float32(DOWN), jnp.float32(0.0))
        block = tiles_ref[0, 0, at].astype(f32) * factor
        i, j = (p // col_tiles) * tile, (p % col_tiles) * tile
        a_ref[i : i + tile, j : j + tile] = block.astype(bf16)
        at_ref[j : j + tile, i : i + tile] = block.T.astype(bf16)

    def fold(ref, at, factor, op):
        part = ref[at : at + 128, :].astype(f32) * factor
        if op is jnp.add:
            part = part * part
        total = part[:, :128]
        for j in range(128, part.shape[1], 128):
            total = op(total, part[:, j : j + 128])
        return total.T

    def peaks(turn, row, col_up):
        for i in range(0, rows, 128):
            peak = jnp.max(fold(a_ref, i, col_up, jnp.maximum), axis=0, keepdims=True)
            rpeak_s[turn, :, i : i + 128] = peak * row[:, i : i + 128]
        for j in range(0, cols, 128):
            peak = jnp.max(fold(at_ref, j, row, jnp.maximum), axis=0, keepdims=True)
            cpeak_s[turn, :, j : j + 128] = peak * col_up[:, j : j + 128]

    def rpeak_copy(turn, d):
        return pltpu.make_async_remote_copy(
            rpeak_s.at[turn], rpeak_r.at[turn, d], rp_ss.at[turn, d], rp_rs.at[turn, d],
            device_id=roster_peer(d), device_id_type=MESH)

    def cpeak_copy(turn, d):
        return pltpu.make_async_remote_copy(
            cpeak_s.at[turn], cpeak_r.at[turn, d], cp_ss.at[turn, d], cp_rs.at[turn, d],
            device_id=band_peer(d), device_id_type=MESH)

    def peaks_send(turn):
        for d in range(1, nb):
            cpeak_copy(turn, d).start()
        for d in range(1, nr):
            rpeak_copy(turn, d).start()

    def peaks_wait(turn):
        row = rpeak_s[turn]
        col = cpeak_s[turn]
        for d in range(1, nr):
            rpeak_copy(turn, d).wait_recv()
            row = jnp.maximum(row, rpeak_r[turn, d])
        for d in range(1, nb):
            cpeak_copy(turn, d).wait_recv()
            col = jnp.maximum(col, cpeak_r[turn, d])
        return row, col

    def fr_copy(d):
        return pltpu.make_async_remote_copy(
            fr_s, fr_r.at[d], fr_ss.at[d], fr_rs.at[d],
            device_id=roster_peer(d), device_id_type=MESH)

    def fb_copy(d):
        return pltpu.make_async_remote_copy(
            fb_s, fb_r.at[d], fb_ss.at[d], fb_rs.at[d],
            device_id=band_peer(d), device_id_type=MESH)

    is_end = (z == 0) | (z == nb - 1)
    inner = (z > 0) & (z < nb - 1)
    lead = (z * 2) // nb
    back = 1 - lead

    def split_dot(value, matrix):
        high = value.astype(bf16)
        low = (value - high.astype(f32)).astype(bf16)
        both = jnp.dot(jnp.concatenate([high, low], 0), matrix, preferred_element_type=f32)
        return both[: value.shape[0]] + both[value.shape[0] :]

    def g_copy(par, way, k):
        at = pl.ds(k * cs, cs)
        return pltpu.make_async_remote_copy(
            snd.at[way, at], rec.at[par, way, at], g_ss.at[way, k], g_rs.at[par, way, k],
            device_id=((z + nb + 1 - 2 * way) % nb, r), device_id_type=MESH)

    def g_sent(grp, par):
        for k in range(grp * kper, (grp + 1) * kper):
            g_copy(par, lead, k).wait_send()

        @pl.when(inner)
        def _():
            for k in range(grp * kper, (grp + 1) * kper):
                g_copy(par, back, k).wait_send()

    def g_start(grp, t):
        if t > 0:
            g_sent(grp, (t - 1) % 2)
        at = pl.ds(grp * per, per)
        value = split_dot(y_t[at, :], a_ref[...])
        own[at, :] = value

        @pl.when(is_end)
        def _():
            snd[lead, at, :] = value
            for k in range(grp * kper, (grp + 1) * kper):
                g_copy(t % 2, lead, k).start()

    def first(t, k):
        @pl.when(inner)
        def _():
            at = pl.ds(k * cs, cs)
            g_copy(t % 2, lead, k).wait_recv()
            snd[lead, at, :] = rec[t % 2, lead, at, :] + own[at, :]
            g_copy(t % 2, lead, k).start()

    def second(t, k):
        g_copy(t % 2, back, k).wait_recv()

        @pl.when(inner)
        def _():
            at = pl.ds(k * cs, cs)
            snd[back, at, :] = rec[t % 2, back, at, :] + own[at, :]
            g_copy(t % 2, back, k).start()

    def block_at(grp, q):
        if parts == 1:
            return (pl.ds(pl.multiple_of(grp * per + q * bs, 8), bs), slice(None))
        return (
            pl.ds(pl.multiple_of(grp * per + (q // parts) * bs, 8), bs),
            pl.ds(pl.multiple_of((q % parts) * width, 128), width),
        )

    def rs_copy(grp, d):
        return pltpu.make_async_remote_copy(
            hown.at[block_at(grp, (r + d) % nr)], hrec.at[grp, d],
            rs_ss.at[grp, d], rs_rs.at[grp, d],
            device_id=roster_peer(d), device_id_type=MESH)

    def ag_copy(grp, d):
        here = block_at(grp, r)
        return pltpu.make_async_remote_copy(
            y_t.at[here], y_t.at[here], ag_ss.at[grp, d], ag_rs.at[grp, d],
            device_id=roster_peer(d), device_id_type=MESH)

    def ag_arrived(grp, d):
        here = block_at(grp, (r + nr - d) % nr)
        return pltpu.make_async_remote_copy(
            y_t.at[here], y_t.at[here], ag_ss.at[grp, d], ag_rs.at[grp, d],
            device_id=roster_peer(d), device_id_type=MESH)

    order = sorted(range(1, nr), key=lambda d: -bin(d).count("1"))

    one_row = jnp.ones((1, rows), f32)
    one_col = jnp.ones((1, cols), f32)
    row, col_up = one_row, one_col * UP
    peaks(0, row, col_up)
    pl.semaphore_wait(barrier, nr - 1 + nb - 1)
    peaks_send(0)
    for i in range(0, rows, 128):
        y_t[:, i : i + 128] = y0_ref[i : i + 128, :].T
    for grp in range(groups):
        g_start(grp, 0)

    steps = []
    for k in range(groups * kper + skew):
        if k < groups * kper:
            steps.append(functools.partial(first, 0, k))
        if k >= skew:
            steps.append(functools.partial(second, 0, k - skew))
    take = -(-len(steps) // (ROUNDS + 1))
    for turn in range(ROUNDS):
        if turn == 0:
            for j in range(0, cols, 128):
                cost_t[:, j : j + 128] = cost_ref[j : j + 128, :].T
                x_t[:, j : j + 128] = x0_ref[j : j + 128, :].T
        for step in steps[turn * take : (turn + 1) * take]:
            step()
        row_peak, col_peak = peaks_wait(turn)
        row = row / jnp.sqrt(row_peak + eps)
        col_up = col_up / jnp.sqrt(col_peak + eps)
        if turn + 1 < ROUNDS:
            peaks(turn + 1, row, col_up)
            peaks_send(turn + 1)
    col = col_up * DOWN
    row_up = row * UP

    squares = jnp.zeros((1, 128), f32)
    for j in range(0, cols, 128):
        part = jnp.sum(fold(at_ref, j, row, jnp.add), axis=0, keepdims=True)
        scale = col_up[:, j : j + 128]
        squares = squares + part * scale * scale
    fr_s[...] = squares
    for d in range(1, nr):
        fr_copy(d).start()
    for j in range(0, cols, 128):
        cost_t[:, j : j + 128] = cost_t[:, j : j + 128] * col[:, j : j + 128]
    for d in range(1, nr):
        fr_copy(d).wait_recv()
        squares = squares + fr_r[d]
    fb_s[...] = squares
    for d in range(1, nb):
        fb_copy(d).start()
    for step in steps[ROUNDS * take :]:
        step()
    for d in range(1, nb):
        fb_copy(d).wait_recv()
        squares = squares + fb_r[d]
    eta = 0.9 / jnp.sqrt(jnp.sum(squares, axis=1, keepdims=True) + eps)
    eta_col = eta * col
    eta_row = eta * row

    def update(t, k):
        at = pl.ds(k * cs, cs)
        total = snd[lead, at, :] + rec[t % 2, back, at, :]
        before = x_t[at, :]
        after = jnp.clip(before - eta_col * (cost_t[at, :] - col_up * total), 0.0, 1.0)
        x_t[at, :] = after
        u_t[at, :] = 2.0 * after - before

    def h_start(grp, t):
        if t > 0:
            for d in order:
                rs_copy(grp, d).wait_send()
        at = pl.ds(grp * per, per)
        hown[at, :] = split_dot(u_t[at, :], at_ref[...])
        for d in order:
            rs_copy(grp, d).start()

    def h_mid(grp, t):
        here = block_at(grp, r)
        total = hown[here]
        for d in range(1, nr):
            rs_copy(grp, d).wait_recv()
            total = total + hrec[grp, d]
        if t > 0:
            for d in order:
                ag_copy(grp, d).wait_send()
        if parts == 1:
            y_t[here] = y_t[here] + eta_row * (row - row_up * total)
        else:
            lane = (r % parts) * width
            own_row = jnp.zeros((1, width), f32)
            own_eta = jnp.zeros((1, width), f32)
            for q in range(parts):
                mine = lane == q * width
                own_row = jnp.where(mine, row[:, q * width : (q + 1) * width], own_row)
                own_eta = jnp.where(mine, eta_row[:, q * width : (q + 1) * width], own_eta)
            y_t[here] = y_t[here] + own_eta * (own_row - (own_row * UP) * total)
        for d in order:
            ag_copy(grp, d).start()

    def h_fin(grp):
        for d in range(1, nr):
            ag_arrived(grp, d).wait_recv()

    def relays(t, grp, lo, hi):
        for k in range(lo, hi):
            if k < kper:
                first(t, grp * kper + k)
            if k >= skew:
                second(t, grp * kper + k - skew)
                update(t, grp * kper + k - skew)

    for t in range(ITERS):
        if t == 0:
            for k in range(groups * kper):
                update(0, k)
                if (k + 1) % kper == 0:
                    h_start(k // kper, 0)
            for grp in range(groups):
                h_mid(grp, 0)
        elif groups == 1:
            relays(t, 0, 0, kper + skew)
            h_start(0, t)
            h_mid(0, t)
        else:
            relays(t, 0, 0, kper + skew)
            h_start(0, t)
            relays(t, 1, 0, kper)
            h_mid(0, t)
            relays(t, 1, kper, kper + skew)
            h_start(1, t)
            if t + 1 < ITERS:
                h_fin(0)
                g_start(0, t + 1)
            h_mid(1, t)
        for grp in range(groups):
            if t + 1 == ITERS:
                h_fin(grp)
            elif groups == 1 or t == 0 or grp > 0:
                h_fin(grp)
                g_start(grp, t + 1)

    for j in range(0, cols, 128):
        primal_ref[j : j + 128, :] = (x_t[:, j : j + 128] / col[:, j : j + 128]).T
    for i in range(0, rows, 128):
        dual_ref[i : i + 128, :] = (y_t[:, i : i + 128] / row[:, i : i + 128]).T

    for grp in range(groups):
        g_sent(grp, (ITERS - 1) % 2)
        for d in order:
            rs_copy(grp, d).wait_send()
            ag_copy(grp, d).wait_send()
    for d in range(1, nr):
        fr_copy(d).wait_send()
        for turn in range(ROUNDS):
            rpeak_copy(turn, d).wait_send()
    for d in range(1, nb):
        fb_copy(d).wait_send()
        for turn in range(ROUNDS):
            cpeak_copy(turn, d).wait_send()


def shards(nb, nr, tiles, tile_slots, tile_count, costs, primal_start, dual_start):
    rows, scen = dual_start.shape
    cols = costs.shape[0]
    groups = GROUPS if (scen // GROUPS) * rows // nr >= 1024 else 1
    cs = CHUNK
    chunks = scen // cs
    per = scen // groups
    bs = max(8, per // nr)
    width = per * rows // (nr * bs)
    vmem = pl.BlockSpec(memory_space=pltpu.VMEM)
    smem = pl.BlockSpec(memory_space=pltpu.SMEM)
    dma = pltpu.SemaphoreType.DMA
    return pl.pallas_call(
        functools.partial(kernel, (nb, nr, groups, cs, SKEW)),
        name="primal_dual",
        out_shape=(
            jax.ShapeDtypeStruct((cols, scen), f32),
            jax.ShapeDtypeStruct((rows, scen), f32),
        ),
        in_specs=[smem, smem, vmem, vmem, vmem, vmem],
        out_specs=(vmem, vmem),
        scratch_shapes=[
            pltpu.VMEM((rows, cols), bf16),
            pltpu.VMEM((cols, rows), bf16),
            pltpu.VMEM((scen, cols), f32),
            pltpu.VMEM((scen, cols), f32),
            pltpu.VMEM((scen, cols), f32),
            pltpu.VMEM((scen, rows), f32),
            pltpu.VMEM((scen, cols), f32),
            pltpu.VMEM((2, scen, cols), f32),
            pltpu.VMEM((2, 2, scen, cols), f32),
            pltpu.VMEM((scen, rows), f32),
            pltpu.VMEM((groups, nr, bs, width), f32),
            pltpu.VMEM((ROUNDS, 1, rows), f32),
            pltpu.VMEM((ROUNDS, nr, 1, rows), f32),
            pltpu.VMEM((ROUNDS, 1, cols), f32),
            pltpu.VMEM((ROUNDS, nb, 1, cols), f32),
            pltpu.VMEM((1, 128), f32),
            pltpu.VMEM((nr, 1, 128), f32),
            pltpu.VMEM((1, 128), f32),
            pltpu.VMEM((nb, 1, 128), f32),
            dma((ROUNDS, nr)),
            dma((ROUNDS, nr)),
            dma((ROUNDS, nb)),
            dma((ROUNDS, nb)),
            dma((nr,)),
            dma((nr,)),
            dma((nb,)),
            dma((nb,)),
            dma((2, chunks)),
            dma((2, 2, chunks)),
            dma((groups, nr)),
            dma((groups, nr)),
            dma((groups, nr)),
            dma((groups, nr)),
        ],
        compiler_params=pltpu.CompilerParams(collective_id=0, has_side_effects=True),
    )(tile_slots, tile_count, tiles, costs, primal_start, dual_start)


def solution(mesh):
    placed = (
        P("band", "roster", None, None, None),
        P("band", "roster", None),
        P("band", "roster"),
        P("roster", None),
        P("roster", None),
        P("band", None),
    )
    return jax.shard_map(
        functools.partial(shards, mesh.shape["band"], mesh.shape["roster"]),
        mesh=mesh,
        in_specs=placed,
        out_specs=(P("roster", None), P("band", None)),
        check_vma=False,
    )
```

```python
import functools

import jax
import jax.numpy as jnp
from jax import lax
from jax.experimental import pallas as pl
from jax.experimental.pallas import tpu as pltpu
from jax.sharding import PartitionSpec as P

ROUNDS = 3
ITERS = 4
eps = 1e-06
GROUPS = 2
CHUNK = 16
HOP = 1.7
LINK = 0.066
SUM = 4.4
START = 0.7
ROUND = 2.0
FROB = 6.0
SHIFT = 4.3
DOWN = 2.0**-24
UP = 2.0**24
MESH = pl.DeviceIdType.MESH
f32 = jnp.float32
bf16 = jnp.bfloat16


def kernel(
    cfg, slots_ref, count_ref, tiles_ref, cost_ref, x0_ref, y0_ref, primal_ref, dual_ref,
    a_ref, at_ref, cost_t, x_t, u_t, y_t, own, snd, rec, hown, hrec,
    rpeak_s, rpeak_r, cpeak_s, cpeak_r, fr_s, fr_r, fb_s, fb_r,
    rp_ss, rp_rs, cp_ss, cp_rs, fr_ss, fr_rs, fb_ss, fb_rs,
    g_ss, g_rs, rs_ss, rs_rs, ag_ss, ag_rs,
):
    nb, nr, groups, cs = cfg
    z = lax.axis_index("band")
    r = lax.axis_index("roster")
    slots = tiles_ref.shape[2]
    tile = tiles_ref.shape[3]
    rows, scen = y0_ref.shape
    cols = cost_ref.shape[0]
    col_tiles = cols // tile
    per = scen // groups
    kper = per // cs
    bs = max(8, per // nr)
    width = per * rows // (nr * bs)
    parts = rows // width

    def roster_peer(d):
        return (z, (r + d) % nr)

    def band_peer(d):
        return ((z + d) % nb, r)

    barrier = pltpu.get_barrier_semaphore()
    for d in range(1, nr):
        pl.semaphore_signal(barrier, inc=1, device_id=roster_peer(d), device_id_type=MESH)
    for d in range(1, nb):
        pl.semaphore_signal(barrier, inc=1, device_id=band_peer(d), device_id_type=MESH)

    for p in range(slots):
        at = jnp.int32(0)
        for s in range(slots):
            at = jnp.where(slots_ref[0, 0, s] == p, jnp.int32(s), at)
        factor = jnp.where(at < count_ref[0, 0], jnp.float32(DOWN), jnp.float32(0.0))
        block = tiles_ref[0, 0, at].astype(f32) * factor
        i, j = (p // col_tiles) * tile, (p % col_tiles) * tile
        a_ref[i : i + tile, j : j + tile] = block.astype(bf16)
        at_ref[j : j + tile, i : i + tile] = block.T.astype(bf16)

    def fold(ref, at, factor, op):
        part = ref[at : at + 128, :].astype(f32) * factor
        if op is jnp.add:
            part = part * part
        total = part[:, :128]
        for j in range(128, part.shape[1], 128):
            total = op(total, part[:, j : j + 128])
        return total.T

    def peaks(turn, row, col_up):
        for i in range(0, rows, 128):
            peak = jnp.max(fold(a_ref, i, col_up, jnp.maximum), axis=0, keepdims=True)
            rpeak_s[turn, :, i : i + 128] = peak * row[:, i : i + 128]
        for j in range(0, cols, 128):
            peak = jnp.max(fold(at_ref, j, row, jnp.maximum), axis=0, keepdims=True)
            cpeak_s[turn, :, j : j + 128] = peak * col_up[:, j : j + 128]

    def rpeak_copy(turn, d):
        return pltpu.make_async_remote_copy(
            rpeak_s.at[turn], rpeak_r.at[turn, d], rp_ss.at[turn, d], rp_rs.at[turn, d],
            device_id=roster_peer(d), device_id_type=MESH)

    def cpeak_copy(turn, d):
        return pltpu.make_async_remote_copy(
            cpeak_s.at[turn], cpeak_r.at[turn, d], cp_ss.at[turn, d], cp_rs.at[turn, d],
            device_id=band_peer(d), device_id_type=MESH)

    def peaks_send(turn):
        for d in range(1, nb):
            cpeak_copy(turn, d).start()
        for d in range(1, nr):
            rpeak_copy(turn, d).start()

    def peaks_wait(turn):
        row = rpeak_s[turn]
        col = cpeak_s[turn]
        for d in range(1, nr):
            rpeak_copy(turn, d).wait_recv()
            row = jnp.maximum(row, rpeak_r[turn, d])
        for d in range(1, nb):
            cpeak_copy(turn, d).wait_recv()
            col = jnp.maximum(col, cpeak_r[turn, d])
        return row, col

    def fr_copy(d):
        return pltpu.make_async_remote_copy(
            fr_s, fr_r.at[d], fr_ss.at[d], fr_rs.at[d],
            device_id=roster_peer(d), device_id_type=MESH)

    def fb_copy(d):
        return pltpu.make_async_remote_copy(
            fb_s, fb_r.at[d], fb_ss.at[d], fb_rs.at[d],
            device_id=band_peer(d), device_id_type=MESH)

    is_end = (z == 0) | (z == nb - 1)
    inner = (z > 0) & (z < nb - 1)
    lead = (z * 2) // nb
    back = 1 - lead

    def split_dot(value, matrix):
        high = value.astype(bf16)
        low = (value - high.astype(f32)).astype(bf16)
        both = jnp.dot(jnp.concatenate([high, low], 0), matrix, preferred_element_type=f32)
        return both[: value.shape[0]] + both[value.shape[0] :]

    def g_copy(par, way, k):
        at = pl.ds(k * cs, cs)
        return pltpu.make_async_remote_copy(
            snd.at[way, at], rec.at[par, way, at], g_ss.at[way, k], g_rs.at[par, way, k],
            device_id=((z + nb + 1 - 2 * way) % nb, r), device_id_type=MESH)

    def g_sent(grp, par):
        for k in range(grp * kper, (grp + 1) * kper):
            g_copy(par, lead, k).wait_send()

        @pl.when(inner)
        def _():
            for k in range(grp * kper, (grp + 1) * kper):
                g_copy(par, back, k).wait_send()

    def g_start(grp, t):
        if t > 0:
            g_sent(grp, (t - 1) % 2)
        at = pl.ds(grp * per, per)
        value = split_dot(y_t[at, :], a_ref[...])
        own[at, :] = value

        @pl.when(is_end)
        def _():
            snd[lead, at, :] = value
            for k in range(grp * kper, (grp + 1) * kper):
                g_copy(t % 2, lead, k).start()

    def first(t, k):
        @pl.when(inner)
        def _():
            at = pl.ds(k * cs, cs)
            g_copy(t % 2, lead, k).wait_recv()
            snd[lead, at, :] = rec[t % 2, lead, at, :] + own[at, :]
            g_copy(t % 2, lead, k).start()

    def second(t, k):
        g_copy(t % 2, back, k).wait_recv()

        @pl.when(inner)
        def _():
            at = pl.ds(k * cs, cs)
            snd[back, at, :] = rec[t % 2, back, at, :] + own[at, :]
            g_copy(t % 2, back, k).start()

    def block_at(grp, q):
        if parts == 1:
            return (pl.ds(pl.multiple_of(grp * per + q * bs, 8), bs), slice(None))
        return (
            pl.ds(pl.multiple_of(grp * per + (q // parts) * bs, 8), bs),
            pl.ds(pl.multiple_of((q % parts) * width, 128), width),
        )

    def rs_copy(grp, d):
        return pltpu.make_async_remote_copy(
            hown.at[block_at(grp, (r + d) % nr)], hrec.at[grp, d],
            rs_ss.at[grp, d], rs_rs.at[grp, d],
            device_id=roster_peer(d), device_id_type=MESH)

    def ag_copy(grp, d):
        here = block_at(grp, r)
        return pltpu.make_async_remote_copy(
            y_t.at[here], y_t.at[here], ag_ss.at[grp, d], ag_rs.at[grp, d],
            device_id=roster_peer(d), device_id_type=MESH)

    def ag_arrived(grp, d):
        here = block_at(grp, (r + nr - d) % nr)
        return pltpu.make_async_remote_copy(
            y_t.at[here], y_t.at[here], ag_ss.at[grp, d], ag_rs.at[grp, d],
            device_id=roster_peer(d), device_id_type=MESH)

    order = sorted(range(1, nr), key=lambda d: -bin(d).count("1"))

    one_row = jnp.ones((1, rows), f32)
    one_col = jnp.ones((1, cols), f32)
    row, col_up = one_row, one_col * UP
    peaks(0, row, col_up)
    pl.semaphore_wait(barrier, nr - 1 + nb - 1)
    peaks_send(0)
    for i in range(0, rows, 128):
        y_t[:, i : i + 128] = y0_ref[i : i + 128, :].T
    for grp in range(groups):
        g_start(grp, 0)

    state = dict(row=row, col_up=col_up)

    def equilibrate(turn):
        if turn == 0:
            for j in range(0, cols, 128):
                cost_t[:, j : j + 128] = cost_ref[j : j + 128, :].T
                x_t[:, j : j + 128] = x0_ref[j : j + 128, :].T
        row_peak, col_peak = peaks_wait(turn)
        state["row"] = state["row"] / jnp.sqrt(row_peak + eps)
        state["col_up"] = state["col_up"] / jnp.sqrt(col_peak + eps)
        if turn + 1 < ROUNDS:
            peaks(turn + 1, state["row"], state["col_up"])
            peaks_send(turn + 1)
        else:
            squares_start()

    def squares_start():
        row, col_up = state["row"], state["col_up"]
        col = state["col"] = col_up * DOWN
        state["row_up"] = row * UP
        squares = jnp.zeros((1, 128), f32)
        for j in range(0, cols, 128):
            part = jnp.sum(fold(at_ref, j, row, jnp.add), axis=0, keepdims=True)
            scale = col_up[:, j : j + 128]
            squares = squares + part * scale * scale
        fr_s[...] = squares
        for d in range(1, nr):
            fr_copy(d).start()
        for j in range(0, cols, 128):
            cost_t[:, j : j + 128] = cost_t[:, j : j + 128] * col[:, j : j + 128]
        state["squares"] = squares

    def squares_mid():
        squares = state["squares"]
        for d in range(1, nr):
            fr_copy(d).wait_recv()
            squares = squares + fr_r[d]
        fb_s[...] = squares
        for d in range(1, nb):
            fb_copy(d).start()
        state["squares"] = squares

    def squares_end():
        squares = state["squares"]
        for d in range(1, nb):
            fb_copy(d).wait_recv()
            squares = squares + fb_r[d]
        eta = 0.9 / jnp.sqrt(jnp.sum(squares, axis=1, keepdims=True) + eps)
        state["eta_col"] = eta * state["col"]
        state["eta_row"] = eta * state["row"]

    def update(t, k):
        at = pl.ds(k * cs, cs)
        total = snd[lead, at, :] + rec[t % 2, back, at, :]
        before = x_t[at, :]
        eta_col, col_up = state["eta_col"], state["col_up"]
        after = jnp.clip(before - eta_col * (cost_t[at, :] - col_up * total), 0.0, 1.0)
        x_t[at, :] = after
        u_t[at, :] = 2.0 * after - before

    def h_start(grp, t):
        if t > 0:
            for d in order:
                rs_copy(grp, d).wait_send()
        at = pl.ds(grp * per, per)
        hown[at, :] = split_dot(u_t[at, :], at_ref[...])
        for d in order:
            rs_copy(grp, d).start()

    def h_mid(grp, t):
        here = block_at(grp, r)
        row, row_up, eta_row = state["row"], state["row_up"], state["eta_row"]
        total = hown[here]
        for d in range(1, nr):
            rs_copy(grp, d).wait_recv()
            total = total + hrec[grp, d]
        if t > 0:
            for d in order:
                ag_copy(grp, d).wait_send()
        if parts == 1:
            y_t[here] = y_t[here] + eta_row * (row - row_up * total)
        else:
            lane = (r % parts) * width
            own_row = jnp.zeros((1, width), f32)
            own_eta = jnp.zeros((1, width), f32)
            for q in range(parts):
                mine = lane == q * width
                own_row = jnp.where(mine, row[:, q * width : (q + 1) * width], own_row)
                own_eta = jnp.where(mine, eta_row[:, q * width : (q + 1) * width], own_eta)
            y_t[here] = y_t[here] + own_eta * (own_row - (own_row * UP) * total)
        for d in order:
            ag_copy(grp, d).start()

    def h_fin(grp):
        for d in range(1, nr):
            ag_arrived(grp, d).wait_recv()

    plan = []

    def put(when, step, *args):
        plan.append((when, len(plan), functools.partial(step, *args)))

    unit = LINK * cs
    for turn in range(ROUNDS):
        put(ROUND * (turn + 1), equilibrate, turn)
    put(ROUND * ROUNDS + FROB / 2, squares_mid)
    ready = ROUND * ROUNDS + FROB
    put(ready, squares_end)
    for grp in range(groups):
        ks = range(grp * kper, (grp + 1) * kper)
        for k in ks:
            put(START + unit * (k + 1) + HOP, first, 0, k)
            put(START + unit * (k + 2) + 2 * HOP, second, 0, k)
        begin = max(ready, START + unit * (kper + 2) + 3 * HOP) + grp * SHIFT
        for t in range(ITERS):
            if t > 0:
                for i, k in enumerate(ks):
                    put(begin + unit * (i + 1) + HOP, first, t, k)
                    put(begin + unit * (i + 2) + 2 * HOP, second, t, k)
                    put(begin + unit * (i + 2) + 2 * HOP, update, t, k)
                begin = begin + unit * (kper + 2) + 3 * HOP
            else:
                for k in ks:
                    put(begin, update, t, k)
            put(begin, h_start, grp, t)
            put(begin + SUM, h_mid, grp, t)
            put(begin + 2 * SUM, h_fin, grp)
            if t + 1 < ITERS:
                put(begin + 2 * SUM, g_start, grp, t + 1)
            begin = begin + 2 * SUM + START
    for when, index, step in sorted(plan, key=lambda entry: entry[:2]):
        step()
    row, col = state["row"], state["col"]

    for j in range(0, cols, 128):
        primal_ref[j : j + 128, :] = (x_t[:, j : j + 128] / col[:, j : j + 128]).T
    for i in range(0, rows, 128):
        dual_ref[i : i + 128, :] = (y_t[:, i : i + 128] / row[:, i : i + 128]).T

    for grp in range(groups):
        g_sent(grp, (ITERS - 1) % 2)
        for d in order:
            rs_copy(grp, d).wait_send()
            ag_copy(grp, d).wait_send()
    for d in range(1, nr):
        fr_copy(d).wait_send()
        for turn in range(ROUNDS):
            rpeak_copy(turn, d).wait_send()
    for d in range(1, nb):
        fb_copy(d).wait_send()
        for turn in range(ROUNDS):
            cpeak_copy(turn, d).wait_send()


def shards(nb, nr, tiles, tile_slots, tile_count, costs, primal_start, dual_start):
    rows, scen = dual_start.shape
    cols = costs.shape[0]
    groups = GROUPS if (scen // GROUPS) * rows // nr >= 1024 else 1
    cs = CHUNK
    chunks = scen // cs
    per = scen // groups
    bs = max(8, per // nr)
    width = per * rows // (nr * bs)
    vmem = pl.BlockSpec(memory_space=pltpu.VMEM)
    smem = pl.BlockSpec(memory_space=pltpu.SMEM)
    dma = pltpu.SemaphoreType.DMA
    return pl.pallas_call(
        functools.partial(kernel, (nb, nr, groups, cs)),
        name="primal_dual",
        out_shape=(
            jax.ShapeDtypeStruct((cols, scen), f32),
            jax.ShapeDtypeStruct((rows, scen), f32),
        ),
        in_specs=[smem, smem, vmem, vmem, vmem, vmem],
        out_specs=(vmem, vmem),
        scratch_shapes=[
            pltpu.VMEM((rows, cols), bf16),
            pltpu.VMEM((cols, rows), bf16),
            pltpu.VMEM((scen, cols), f32),
            pltpu.VMEM((scen, cols), f32),
            pltpu.VMEM((scen, cols), f32),
            pltpu.VMEM((scen, rows), f32),
            pltpu.VMEM((scen, cols), f32),
            pltpu.VMEM((2, scen, cols), f32),
            pltpu.VMEM((2, 2, scen, cols), f32),
            pltpu.VMEM((scen, rows), f32),
            pltpu.VMEM((groups, nr, bs, width), f32),
            pltpu.VMEM((ROUNDS, 1, rows), f32),
            pltpu.VMEM((ROUNDS, nr, 1, rows), f32),
            pltpu.VMEM((ROUNDS, 1, cols), f32),
            pltpu.VMEM((ROUNDS, nb, 1, cols), f32),
            pltpu.VMEM((1, 128), f32),
            pltpu.VMEM((nr, 1, 128), f32),
            pltpu.VMEM((1, 128), f32),
            pltpu.VMEM((nb, 1, 128), f32),
            dma((ROUNDS, nr)),
            dma((ROUNDS, nr)),
            dma((ROUNDS, nb)),
            dma((ROUNDS, nb)),
            dma((nr,)),
            dma((nr,)),
            dma((nb,)),
            dma((nb,)),
            dma((2, chunks)),
            dma((2, 2, chunks)),
            dma((groups, nr)),
            dma((groups, nr)),
            dma((groups, nr)),
            dma((groups, nr)),
        ],
        compiler_params=pltpu.CompilerParams(collective_id=0, has_side_effects=True),
    )(tile_slots, tile_count, tiles, costs, primal_start, dual_start)


def solution(mesh):
    placed = (
        P("band", "roster", None, None, None),
        P("band", "roster", None),
        P("band", "roster"),
        P("roster", None),
        P("roster", None),
        P("band", None),
    )
    return jax.shard_map(
        functools.partial(shards, mesh.shape["band"], mesh.shape["roster"]),
        mesh=mesh,
        in_specs=placed,
        out_specs=(P("roster", None), P("band", None)),
        check_vma=False,
    )
```
